32 devices in a mesh: group: 2 (over x), area: 16 (over z, y, core).
Axes of the slice: x: 2, y: 2, z: 4, core: 2. Of those that a mesh axis runs over, the one named last changes fastest.
Arguments:
- state_init: float32 [64, 12288], P('group', 'area'), parts along dimension 0, may hold values from -6 to 6
- prior_interval_trace: bfloat16 [4, 64, 12288], P(None, 'group', 'area'), parts along dimension 1, may hold values from -0.8984375 to 0.8984375
- drive_input: bfloat16 [64, 12288], P('group', 'area'), parts along dimension 0, may hold values from -4 to 4
- leak_rate: float32 [24576], P(('group', 'area')), parts along dimension 0, may hold values from 0.15 to 1
- w_recur: bfloat16 [24576, 6144], P(('group', 'area')), parts along dimension 0, may hold values from -0.078125 to 0.078125
- w_send: bfloat16 [24576, 768], P(('group', 'area')), parts along dimension 0, may hold values from -0.078125 to 0.078125
- w_recv: bfloat16 [24576, 768], P(('group', 'area')), parts along dimension 0, may hold values from -0.21875 to 0.21875
- area_mask: int32 [4, 2], P('group'), parts along dimension 0, may hold values 0 or 1
- coupling: float32 [4, 2], P('group'), parts along dimension 0, may hold values from 0.1 to 0.6
- delay_slot: int32 [4, 2], P('group'), parts along dimension 0, may hold values from 0 to 3
Outputs:
- final_state: float32 [64, 12288], P('group', 'area'), parts along dimension 0
- final_history: bfloat16 [4, 64, 12288], P(None, 'group', 'area'), parts along dimension 1
The draws below stay inside these ranges and needn't reach their ends.
There are 2 independent parts, one for each index of `group`. The reference program is written for one: setup_inputs(seed, part) draws one part's arguments, and reference() takes and returns one part's arrays. A program takes and returns all parts, laid end to end along the dimension named above; each array names one. Nothing has to cross between parts.
All inputs are finite; a program needn't handle non-finite values.
Results may differ from the reference program's by a relative error of at most 0.0095.
Values may be sent and summed in bfloat16 or wider, within the bound.
No kernel may reach another device: no remote copies, remote signals or barrier semaphores. Data moves between devices by JAX's collectives and lax.ppermute only.
A program may use at most 64 MiB of HBM per device.

```python
import math
import jax
import jax.numpy as jnp
from jax import lax

NEURONS_REGION = 6144
RANK = 768
LAG_TICKS = 4
INTERVALS = 2
EPISODE_TALLY = 32
REGION_TALLY = 2
ALL_UNITS = 12288


def set_ends(drawn, stream_key, smallest, high):
    longest = drawn.shape.index(max(drawn.shape))
    spots = []
    for shift in (0, 1):
        where = [jax.random.randint(jax.random.fold_in(stream_key, axis), (), 0, length) for axis, length in enumerate(drawn.shape)]
        where[longest] = (where[longest] + shift) % drawn.shape[longest]
        spots.append(tuple(where))
    return drawn.at[spots[0]].set(smallest).at[spots[1]].set(high)


def shard_levels(own_key, shape, shards, least, top_value):
    gain = 1.0
    for axis_at, shards_of in shards:
        heights = jax.random.uniform(jax.random.fold_in(jax.random.fold_in(own_key, 6), axis_at), (shards_of,), jnp.float32, least / len(shards), top_value / len(shards))
        gain = gain * jnp.repeat(jnp.exp(heights), shape[axis_at] // shards_of).reshape((-1,) + (1,) * (len(shape) - 1 - axis_at))
    return gain


def noise(stream_key, shape, deviation, limit, split=(), kind=jnp.bfloat16):
    values = jax.random.normal(stream_key, shape, jnp.float32) * deviation
    if len(split) > 0:
        values = shard_levels(stream_key, shape, split, -0.22, 0.18) * values
    return jnp.clip(values, min=-limit, max=limit).astype(kind)


def setup_inputs(seed: int = 0, part: int = 0) -> dict:
    streams_of = jax.random.split(jax.random.key(seed), 11)
    own_keys = jax.random.split(jax.random.fold_in(streams_of[10], part), 11)
    state_init = noise(own_keys[0], (EPISODE_TALLY, ALL_UNITS), 1.0, 6.0, ((1, 16),), jnp.float32)
    prior_interval_trace = jnp.clip(jax.random.uniform(own_keys[1], (LAG_TICKS, EPISODE_TALLY, ALL_UNITS), jnp.float32, -0.8984375, 0.8984375) * shard_levels(own_keys[1], (LAG_TICKS, EPISODE_TALLY, ALL_UNITS), ((2, 16),), -0.4, 0.0), -0.8984375, 0.8984375).astype(jnp.bfloat16)
    drive_input = noise(own_keys[2], (EPISODE_TALLY, ALL_UNITS), 0.5, 4.0, ((1, 16),))
    leak_rate = jnp.clip(jnp.exp(math.log(1.0) - 1.89712 * jax.random.uniform(own_keys[3], (ALL_UNITS,), jnp.float32) ** shard_levels(own_keys[3], (ALL_UNITS,), ((0, 16),), -0.2, 0.2)), 0.15, 1.0)
    w_recur = noise(own_keys[4], (ALL_UNITS, NEURONS_REGION), NEURONS_REGION ** -0.5, 0.078125, ((0, 16),))
    w_send = noise(own_keys[5], (ALL_UNITS, RANK), NEURONS_REGION ** -0.5, 0.078125, ((0, 16),))
    w_recv = noise(own_keys[6], (ALL_UNITS, RANK), RANK ** -0.5, 0.21875, ((0, 16),))
    area_mask = set_ends((jax.random.randint(own_keys[7], (REGION_TALLY, REGION_TALLY), 0, 2) < 1).astype(jnp.int32), jax.random.fold_in(own_keys[7], 1), 0, 1)
    coupling = jnp.clip(jnp.exp(jax.random.uniform(own_keys[8], (REGION_TALLY, REGION_TALLY), jnp.float32, math.log(0.1), math.log(0.6))), 0.1, 0.6)
    delay_slot = set_ends(jax.random.randint(own_keys[9], (REGION_TALLY, REGION_TALLY), 0, LAG_TICKS), jax.random.fold_in(own_keys[9], 1), 0, LAG_TICKS - 1).astype(jnp.int32)
    return dict(state_init=state_init, prior_interval_trace=prior_interval_trace, drive_input=drive_input, leak_rate=leak_rate, w_recur=w_recur, w_send=w_send, w_recv=w_recv, area_mask=area_mask, coupling=coupling, delay_slot=delay_slot)


def reference(state_init, prior_interval_trace, drive_input, leak_rate, w_recur, w_send, w_recv, area_mask, coupling, delay_slot):
    strength = area_mask.astype(jnp.float32) * coupling
    slots = jnp.arange(LAG_TICKS, dtype=jnp.int32)
    selector = (delay_slot[:, :, None] == slots[None, None, :]).astype(jnp.float32) * strength[:, :, None]
    recur_blocks = w_recur.reshape(REGION_TALLY, NEURONS_REGION, NEURONS_REGION)
    send_blocks = w_send.astype(jnp.float32).reshape(REGION_TALLY, NEURONS_REGION, RANK)
    recv_blocks = w_recv.astype(jnp.float32).reshape(REGION_TALLY, NEURONS_REGION, RANK)

    def remote_input(history):
        spread = history.astype(jnp.float32).reshape(LAG_TICKS, EPISODE_TALLY, REGION_TALLY, NEURONS_REGION)
        readout = jnp.einsum("ktbs,bsr->ktbr", spread, send_blocks, precision=lax.Precision.HIGHEST)
        summed = jnp.einsum("abk,ktbr->atr", selector, readout, precision=lax.Precision.HIGHEST)
        summed = summed.astype(jnp.bfloat16).astype(jnp.float32)
        result = jnp.einsum("atr,aur->tau", summed, recv_blocks, precision=lax.Precision.HIGHEST)
        return result.reshape(EPISODE_TALLY, REGION_TALLY * NEURONS_REGION)

    def one_area(pair):
        rates_area, weights_area = pair
        return jnp.dot(rates_area, weights_area.T, preferred_element_type=jnp.float32)

    def lateral_feedback(spiking_activity):
        sorted_per_region = jnp.transpose(spiking_activity.reshape(EPISODE_TALLY, REGION_TALLY, NEURONS_REGION), (1, 0, 2))
        result = lax.map(one_area, (sorted_per_region, recur_blocks))
        return jnp.transpose(result, (1, 0, 2)).reshape(EPISODE_TALLY, REGION_TALLY * NEURONS_REGION)

    drive = drive_input.astype(jnp.float32)
    neuron_voltage = state_init
    history = prior_interval_trace
    spiking_activity = prior_interval_trace[LAG_TICKS - 1]
    for interval in range(INTERVALS):
        remote = remote_input(history)
        logged_activity = []
        for step_index in range(LAG_TICKS):
            lateral_forcing = lateral_feedback(spiking_activity)
            neuron_voltage = neuron_voltage + leak_rate[None, :] * (-neuron_voltage + lateral_forcing + remote + drive)
            spiking_activity = jnp.tanh(neuron_voltage).astype(jnp.bfloat16)
            logged_activity.append(spiking_activity)
        history = jnp.stack(logged_activity)
    return neuron_voltage, history
```

```python
import jax
import jax.numpy as jnp
from jax import lax
from jax.sharding import PartitionSpec as P

INTERVALS = 2


def flipped(block, mask):
    count = lax.axis_size("area")
    return lax.ppermute(block, "area", [(i, i ^ mask) for i in range(count)])


def times_transposed(rates, weights):
    return lax.dot_general(
        rates, weights, (((1,), (1,)), ((), ())), preferred_element_type=jnp.float32
    )


def body(
    state_init,
    prior_interval_trace,
    drive_input,
    leak_rate,
    w_recur,
    w_send,
    w_recv,
    area_mask,
    coupling,
    delay_slot,
):
    ticks = prior_interval_trace.shape[0]
    trials, units = state_init.shape
    areas = area_mask.shape[1]
    split = lax.axis_size("area") // areas
    position = lax.axis_index("area")
    my_area = position // split
    direct = [2 * chip + 1 for chip in range(1, split // 2)]

    strength = area_mask.astype(jnp.float32) * coupling
    my_strength = lax.dynamic_index_in_dim(strength, my_area, 1, keepdims=False)
    my_slots = lax.dynamic_index_in_dim(delay_slot, my_area, 1, keepdims=False)
    drive = drive_input.astype(jnp.float32)
    leak = leak_rate[None, :]

    def column_block(mask):
        start = ((position ^ mask) % split) * units
        return lax.dynamic_slice_in_dim(w_recur, start, units, 1)

    def readouts(history):
        chosen = []
        for area in range(areas):
            pick = history[0]
            for tick in range(1, ticks):
                pick = jnp.where(my_slots[area] == tick, history[tick], pick)
            chosen.append(pick)
        read = jnp.dot(
            jnp.concatenate(chosen, 0), w_send, preferred_element_type=jnp.float32
        )
        return read.reshape(areas, trials, -1) * my_strength[:, None, None]

    def across_areas(contrib):
        level = areas // 2
        while level:
            half = contrib.shape[0] // 2
            upper = my_area // level % 2 == 1
            keep = jnp.where(upper, contrib[half:], contrib[:half])
            send = jnp.where(upper, contrib[:half], contrib[half:])
            contrib = keep + flipped(send.astype(jnp.bfloat16), split * level | 1)
            level //= 2
        return contrib[0]

    def received(contrib):
        contrib = across_areas(contrib)
        narrow = contrib.astype(jnp.bfloat16)
        for mask in direct:
            contrib = contrib + flipped(narrow, mask)
        contrib = contrib + flipped(contrib.astype(jnp.bfloat16), 1)
        return times_transposed(contrib.astype(jnp.bfloat16), w_recv)

    def recurrent(rates):
        total = times_transposed(rates, column_block(0))
        total = total + times_transposed(flipped(rates, 1), column_block(1))
        for mask in direct:
            there = flipped(rates, mask)
            total = total + times_transposed(there, column_block(mask))
            other = flipped(there, 1)
            total = total + times_transposed(other, column_block(mask ^ 1))
        return total

    potential = state_init
    history = [prior_interval_trace[tick] for tick in range(ticks)]
    rates = history[-1]
    for interval in range(INTERVALS):
        remote = received(readouts(history))
        fixed = remote + drive
        history = []
        for tick in range(ticks):
            potential = potential + leak * (-potential + recurrent(rates) + fixed)
            rates = jnp.tanh(potential).astype(jnp.bfloat16)
            history.append(rates)
    return potential, jnp.stack(history)


def solution(mesh):
    in_specs = (
        P("group", "area"),
        P(None, "group", "area"),
        P("group", "area"),
        P(("group", "area")),
        P(("group", "area"), None),
        P(("group", "area"), None),
        P(("group", "area"), None),
        P("group", None),
        P("group", None),
        P("group", None),
    )
    out_specs = (P("group", "area"), P(None, "group", "area"))
    return jax.shard_map(body, mesh=mesh, in_specs=in_specs, out_specs=out_specs, check_vma=False)
```
